128 devices in a mesh: row: 4 (over x_lo, core), col: 8 (over x_hi, y), tm: 4 (over z).
Axes of the slice: x: 4 (x_hi: 2, x_lo: 2; x = x_hi * 2 + x_lo), y: 4, z: 4, core: 2. Of those that a mesh axis runs over, the one named last changes fastest.
Arguments:
- right_sides: bfloat16 [8, 256, 16384], P(None, 'tm', ('row', 'col')), may hold values from -6 to 6
- eigen_basis: bfloat16 [16384, 16384], P('row', 'col'), may hold values from -0.046875 to 0.046875
- space_values: float32 [16384], P('col'), may hold values from 0.02 to 4
- time_basis: bfloat16 [256, 256], replicated, may hold values from -0.375 to 0.375
- time_values: float32 [256], replicated, may hold values from 0.05 to 4
- noise_level: float32 [1], replicated, may hold values from 0.05 to 0.5
Outputs:
- solved: float32 [8, 256, 16384], P(None, 'tm', ('row', 'col'))
The draws below stay inside these ranges and needn't reach their ends.
All inputs are finite; a program needn't handle non-finite values.
Results may differ from the reference program's by a relative error of at most 0.0037.
Values may be sent and summed in bfloat16 or wider, within the bound.
No kernel may reach another device: no remote copies, remote signals or barrier semaphores. Data moves between devices by JAX's collectives and lax.ppermute only.
A program may use at most 128 MiB of HBM per device.

```python
import math
import jax
import jax.numpy as jnp

NS = 16384
NT = 256
RHS = 8


def shard_levels(key, dims, pieces, low, high):
    factor_of, own = 1.0, jax.random.fold_in(key, 6)
    for dim, parts in pieces:
        steps = jnp.exp(jax.random.uniform(jax.random.fold_in(own, dim), (parts,), jnp.float32, low / len(pieces), high / len(pieces)))
        factor_of = factor_of * jnp.repeat(steps, dims[dim] // parts).reshape([-1 if axis == dim else 1 for axis in range(len(dims))])
    return factor_of


def normal_values(own_key, dims, spread, reach, pieces=(), held_as=jnp.bfloat16):
    entries = jax.random.normal(own_key, dims, jnp.float32) * spread
    if len(pieces) > 0:
        entries = shard_levels(own_key, dims, pieces, -0.22, 0.18) * entries
    return jnp.clip(entries, min=-reach, max=reach).astype(held_as)


def setup_inputs(seed: int = 0) -> dict:
    streams_of = jax.random.split(jax.random.key(seed), 7)
    right_sides = normal_values(streams_of[0], (RHS, NT, NS), 1.0, 6.0, ((1, 4), (2, 32)))
    eigen_basis = normal_values(streams_of[1], (NS, NS), NS ** -0.5, 0.046875, ((0, 4), (1, 8)))
    space_values = jnp.clip(jnp.exp(math.log(4.0) - 5.2983174 * jax.random.uniform(streams_of[2], (NS,), jnp.float32) ** shard_levels(streams_of[2], (NS,), ((0, 8),), -0.2, 0.2)), 0.02, 4.0)
    time_basis = normal_values(streams_of[3], (NT, NT), NT ** -0.5, 0.375)
    time_values = jnp.clip(jnp.exp(jax.random.uniform(streams_of[4], (NT,), jnp.float32, math.log(0.05), math.log(4.0))), 0.05, 4.0)
    noise_level = jnp.clip(jax.random.uniform(streams_of[5], (1,), jnp.float32, 0.05, 0.5), 0.05, 0.5)
    return {"right_sides": right_sides, "eigen_basis": eigen_basis, "space_values": space_values, "time_basis": time_basis, "time_values": time_values, "noise_level": noise_level}


def reference(right_sides, eigen_basis, space_values, time_basis, time_values, noise_level):
    flat = right_sides.reshape(RHS * NT, NS)
    spectral = jnp.dot(flat, eigen_basis, preferred_element_type=jnp.float32).astype(jnp.bfloat16)
    spectral = spectral.reshape(RHS, NT, NS)
    mixed = jnp.einsum("tj,rti->rji", time_basis.astype(jnp.float32), spectral.astype(jnp.float32))
    denom = space_values[None, None, :] * time_values[None, :, None] + noise_level[0]
    scaled = (mixed / denom).astype(jnp.bfloat16)
    back_time = jnp.einsum("tj,rji->rti", time_basis.astype(jnp.float32), scaled.astype(jnp.float32)).astype(jnp.bfloat16)
    solved = jnp.dot(back_time.reshape(RHS * NT, NS), eigen_basis.T, preferred_element_type=jnp.float32)
    return solved.reshape(RHS, NT, NS)
```

```python
import jax
import jax.numpy as jnp
from jax import lax
from jax.sharding import PartitionSpec as P

F32, BF16 = jnp.float32, jnp.bfloat16


def shards(right_sides, eigen_basis, space_values, time_basis, time_values, noise_level):
    rhs, nt, ns = right_sides.shape
    rows = rhs * nt
    basis = space_values.shape[0]
    row, col, tm = lax.axis_index("row"), lax.axis_index("col"), lax.axis_index("tm")
    x_lo, core, x_hi, y = row // 2, row % 2, col // 4, col % 4
    quarter = basis // 4

    def across_x(a):
        return lax.ppermute(a, "col", [(c, c ^ 4) for c in range(8)])

    def along_y(a, k):
        return lax.ppermute(a, "col", [(c, (c & 4) | ((c + k) & 3)) for c in range(8)])

    def along_z(a, k):
        return lax.ppermute(a, "tm", [(z, (z + k) & 3) for z in range(4)])

    def other_core(a):
        return lax.ppermute(a, "row", [(r, r ^ 1) for r in range(4)])

    def other_x(a):
        return lax.ppermute(a, "row", [(r, r ^ 2) for r in range(4)])

    def block(flip, step):
        at = (x_hi ^ flip) * 4 + ((y + step) & 3)
        return lax.dynamic_slice_in_dim(eigen_basis, at * ns, ns, 0)

    def project(a, flip, step):
        return lax.dot_general(
            a, block(flip, step), (((1,), (0,)), ((), ())), preferred_element_type=F32
        )

    own = right_sides.reshape(rows, ns)
    x0 = across_x(own)
    up, down = along_y(own, 1), along_y(own, -1)
    far = along_y(own, 2)
    total = project(own, 0, 0)
    total = total + project(up, 0, -1)
    total = total + project(down, 0, 1)
    x_up, x_down = along_y(x0, 1), along_y(x0, -1)
    total = total + project(x0, 1, 0)
    total = total + project(far, 0, 2)
    x_far = across_x(far)
    total = total + project(x_up, 1, -1)
    total = total + project(x_down, 1, 1)
    total = total + project(x_far, 1, 2)

    parts = total.reshape(2, 2, rhs // 4, nt, basis)
    pick = lax.dynamic_index_in_dim
    got = other_core(pick(parts, 1 - core, 1, False).astype(BF16))
    pair = pick(parts, core, 1, False) + got.astype(F32)
    got = other_x(pick(pair, 1 - x_lo, 0, False).astype(BF16))
    spectral = (pick(pair, x_lo, 0, False) + got.astype(F32)).astype(BF16)

    def lanes(a, z):
        return lax.dynamic_slice_in_dim(a, (z & 3) * quarter, quarter, a.ndim - 1)

    times = [lanes(spectral, tm)] + [along_z(lanes(spectral, tm + k), k) for k in (1, 2, 3)]
    times = jnp.concatenate(times, axis=1)
    turned = jnp.concatenate(
        [lax.dynamic_slice_in_dim(time_basis, ((tm - k) & 3) * nt, nt, 0) for k in range(4)], axis=0
    )
    mixed = jnp.einsum("tj,kti->kji", turned, times, preferred_element_type=F32)
    denom = lanes(space_values, tm)[None, None, :] * time_values[None, :, None] + noise_level[0]
    scaled = (mixed / denom).astype(BF16)
    back = jnp.einsum("tj,kji->kti", turned, scaled, preferred_element_type=F32).astype(BF16)
    pieces = [back[:, :nt]] + [along_z(back[:, k * nt : (k + 1) * nt], -k) for k in (1, 2, 3)]
    mine = jnp.zeros(spectral.shape, BF16)
    for k in range(4):
        mine = lax.dynamic_update_slice_in_dim(mine, pieces[k], ((tm + k) & 3) * quarter, 2)

    c1, c2 = other_core(mine), other_x(mine)
    c3 = other_core(c2)
    fields = jnp.zeros((4,) + mine.shape, BF16)
    for a, at in ((mine, row), (c1, row ^ 1), (c2, row ^ 2), (c3, row ^ 3)):
        fields = lax.dynamic_update_index_in_dim(fields, a, at, 0)
    fields = fields.reshape(rows, basis)

    def expand(flip, step):
        return lax.dot_general(
            fields, block(flip, step), (((1,), (1,)), ((), ())), preferred_element_type=F32
        )

    s_up = along_y(expand(1, 1).astype(BF16), 1)
    s_down = along_y(expand(1, -1).astype(BF16), -1)
    s_far = across_x(expand(1, 2).astype(BF16))
    o_up = along_y(expand(0, 1).astype(BF16), 1)
    o_down = along_y(expand(0, -1).astype(BF16), -1)
    o_x = across_x((expand(1, 0) + s_up.astype(F32) + s_down.astype(F32)).astype(BF16))
    o_far = along_y((expand(0, 2) + s_far.astype(F32)).astype(BF16), 2)
    out = expand(0, 0)
    for a in (o_up, o_down, o_x, o_far):
        out = out + a.astype(F32)
    return out.reshape(rhs, nt, ns)


def solution(mesh):
    placed = (P(None, "tm", ("row", "col")), P("row", "col"), P("col"), P(), P(), P())
    return jax.shard_map(
        shards, mesh=mesh, in_specs=placed, out_specs=P(None, "tm", ("row", "col")), check_vma=False
    )
```

```python
import functools
import jax
import jax.numpy as jnp
from jax import lax
from jax.experimental import pallas as pl
from jax.experimental.pallas import tpu as pltpu
from jax.sharding import PartitionSpec as P

F32, BF16 = jnp.float32, jnp.bfloat16
COST = pl.CostEstimate(flops=1 << 10, transcendentals=0, bytes_accessed=1 << 10)
PARAMS = pltpu.CompilerParams(vmem_limit_bytes=4 << 20)
VMEM = pl.BlockSpec(memory_space=pltpu.VMEM)
SMEM = pl.BlockSpec(memory_space=pltpu.SMEM)


OWN, UP, DOWN, FAR, X_OWN, X_UP, X_DOWN, X_FAR = range(8)


def after(a, *others):
    return lax.optimization_barrier((a, *others))[0]


def rows_at(at_ref, i, ns):
    return pl.ds(pl.multiple_of(at_ref[i] * ns, ns), ns)


def project_kernel(which, final, has_total, at_ref, *refs):
    n = len(which)
    blocks, table, rest = refs[:n], refs[n], refs[n + 1 :]
    m, ns = blocks[0].shape
    width = table.shape[1]
    tile = width // 4
    for j in range(4):
        if final:
            from_lane = pl.multiple_of(((at_ref[8] + j) & 3) * tile, tile)
        else:
            from_lane = j * tile
        lanes = pl.ds(from_lane, tile)
        total = rest[0][:, lanes] if has_total else None
        for i, a in zip(which, blocks):
            term = jnp.dot(a[...], table[rows_at(at_ref, i, ns), lanes], preferred_element_type=F32)
            total = term if total is None else total + term
        to = slice(j * tile, (j + 1) * tile)
        if final:
            rest[-2][:, to] = total[: m // 2].astype(BF16)
            rest[-1][:, to] = total[m // 2 :]
        else:
            rest[-1][:, to] = total


def project(blocks, which, at, table, total=None, final=False):
    m, width = blocks[0].shape[0], table.shape[1]
    args = [at, *blocks, table] + ([] if total is None else [total])
    if final:
        out_shape = [
            jax.ShapeDtypeStruct((m // 2, width), BF16),
            jax.ShapeDtypeStruct((m // 2, width), F32),
        ]
    else:
        out_shape = jax.ShapeDtypeStruct((m, width), F32)
    return pl.pallas_call(
        functools.partial(project_kernel, which, final, total is not None),
        in_specs=[SMEM] + [VMEM] * (len(args) - 1),
        out_specs=[VMEM, VMEM] if final else VMEM,
        out_shape=out_shape,
        input_output_aliases={} if final or total is None else {len(args) - 1: 0},
        cost_estimate=COST,
        compiler_params=PARAMS,
        name="project",
    )(*args)


def first_kernel(at_ref, a_ref, basis_ref, table, total, sems):
    tile = table.shape[1] // 4
    copies = []
    for j in range(4):
        lanes = slice(j * tile, (j + 1) * tile)
        copies.append(pltpu.make_async_copy(basis_ref.at[:, lanes], table.at[:, lanes], sems.at[j]))
        copies[-1].start()
    for j in range(4):
        lanes = slice(j * tile, (j + 1) * tile)
        copies[j].wait()
        rows = rows_at(at_ref, OWN, a_ref.shape[1])
        total[:, lanes] = jnp.dot(a_ref[...], table[rows, lanes], preferred_element_type=F32)


def project_first(a, at, basis):
    return pl.pallas_call(
        first_kernel,
        in_specs=[SMEM, VMEM, pl.BlockSpec(memory_space=pl.ANY)],
        out_specs=[VMEM, VMEM],
        out_shape=[
            pltpu.VMEM(basis.shape, basis.dtype),
            jax.ShapeDtypeStruct((a.shape[0], basis.shape[1]), F32),
        ],
        scratch_shapes=[pltpu.SemaphoreType.DMA((4,))],
        cost_estimate=COST,
        compiler_params=PARAMS,
        name="project_first",
    )(at, a, basis)


def load_kernel(go_ref, basis_ref, table, done, sem):
    copy = pltpu.make_async_copy(basis_ref, table, sem)
    copy.start()
    done[...] = go_ref[0, :8, :128]
    copy.wait()


def load(basis, go):
    return pl.pallas_call(
        load_kernel,
        in_specs=[VMEM, pl.BlockSpec(memory_space=pl.ANY)],
        out_specs=[VMEM, VMEM],
        out_shape=[
            pltpu.VMEM(basis.shape, basis.dtype),
            jax.ShapeDtypeStruct((8, 128), go.dtype),
        ],
        scratch_shapes=[pltpu.SemaphoreType.DMA(())],
        cost_estimate=COST,
        compiler_params=PARAMS,
        name="load",
    )(go, basis)


def expand_kernel(which, ns, n, adds, at_ref, *refs):
    fields, table, refs = refs[:n], refs[n], refs[n + 1 :]
    m = fields[0].shape[0]
    for i, out in zip(which, refs[n * adds :]):
        for h, a in enumerate(fields):
            value = lax.dot_general(
                a[...],
                table[rows_at(at_ref, i, ns), :],
                (((1,), (1,)), ((), ())),
                preferred_element_type=F32,
            )
            for add in refs[h * adds : (h + 1) * adds]:
                value = value + add[...].astype(F32)
            out[h * m : (h + 1) * m, :] = value.astype(out.dtype)


def expand(fields, which, at, table, ns, adds=(), dtype=BF16):
    rows = sum(a.shape[0] for a in fields)
    flat = [a for group in adds for a in group]
    out = pl.pallas_call(
        functools.partial(expand_kernel, which, ns, len(fields), len(flat) // len(fields)),
        in_specs=[SMEM] + [VMEM] * (len(fields) + 1 + len(flat)),
        out_specs=[VMEM] * len(which),
        out_shape=[jax.ShapeDtypeStruct((rows, ns), dtype)] * len(which),
        cost_estimate=COST,
        compiler_params=PARAMS,
        name="expand",
    )(at, *fields, table, *flat)
    return out if len(which) > 1 else out[0]


def filter_kernel(at_ref, noise, space, time, turn, *refs):
    ins, outs, held = refs[:4], refs[4:8], refs[8]
    pair, nt, width = ins[0].shape
    z = at_ref[8]
    for k in range(4):
        rows = pl.ds(pl.multiple_of(((z - k) & 3) * nt, nt), nt)
        for r in range(pair):
            held[rows, r * width : (r + 1) * width] = ins[k][r]
    mixed = lax.dot_general(
        turn[...], held[...], (((0,), (0,)), ((), ())), preferred_element_type=F32
    )
    value = space[:, pl.ds(pl.multiple_of(z * width, width), width)]
    denom = value * time[...] + noise[0]
    scaled = mixed / jnp.concatenate([denom] * pair, axis=1)
    held[...] = jnp.dot(
        turn[...], scaled.astype(BF16), preferred_element_type=F32
    ).astype(BF16)
    for k in range(4):
        rows = pl.ds(pl.multiple_of(((z - k) & 3) * nt, nt), nt)
        for r in range(pair):
            outs[k][r] = held[rows, r * width : (r + 1) * width]


def time_filter(parts, at, noise, space, time, turn):
    pair, nt, width = parts[0].shape
    return pl.pallas_call(
        filter_kernel,
        in_specs=[SMEM, SMEM] + [VMEM] * 7,
        out_specs=[VMEM] * 4,
        out_shape=[jax.ShapeDtypeStruct((pair, nt, width), BF16)] * 4,
        scratch_shapes=[pltpu.VMEM((4 * nt, pair * width), BF16)],
        cost_estimate=COST,
        compiler_params=PARAMS,
        name="time_filter",
    )(at, noise, space[None, :], time[:, None], turn, *parts)


def finish_kernel(rows, at_ref, total, *refs):
    g, out = at_ref[9], refs[-1]
    value = total[...]
    for a in refs[:-1]:
        value = value + a[...].astype(F32)
    for k in range(4):
        to = pl.ds(pl.multiple_of((g ^ k) * rows, rows), rows)
        out[to, :] = value[k * rows : (k + 1) * rows]


def finish(total, at, adds):
    return pl.pallas_call(
        functools.partial(finish_kernel, total.shape[0] // 4),
        in_specs=[SMEM] + [VMEM] * (1 + len(adds)),
        out_specs=VMEM,
        out_shape=jax.ShapeDtypeStruct(total.shape, F32),
        cost_estimate=COST,
        compiler_params=PARAMS,
        name="finish",
    )(at, total, *adds)


def shards(right_sides, eigen_basis, space_values, time_basis, time_values, noise_level):
    rhs, nt, ns = right_sides.shape
    rows = rhs * nt
    basis = space_values.shape[0]
    row, col, tm = lax.axis_index("row"), lax.axis_index("col"), lax.axis_index("tm")
    core, x_hi, y = row & 1, col & 4, col & 3
    quarter = basis // 4
    pair = rhs // 4
    eigen_basis = pltpu.with_memory_space_constraint(eigen_basis, pltpu.HBM)

    def across_x(a):
        with jax.named_scope("across_x"):
            return lax.ppermute(a, "col", [(c, c ^ 4) for c in range(8)])

    def along_y(a, k):
        with jax.named_scope("along_y%d" % (k & 3)):
            return lax.ppermute(a, "col", [(c, (c & 4) | ((c + k) & 3)) for c in range(8)])

    def along_z(a, k):
        with jax.named_scope("along_z%d" % (k & 3)):
            return lax.ppermute(a, "tm", [(z, (z + k) & 3) for z in range(4)])

    def other_core(a):
        with jax.named_scope("other_core"):
            return lax.ppermute(a, "row", [(r, r ^ 1) for r in range(4)])

    def other_x(a):
        with jax.named_scope("other_x"):
            return lax.ppermute(a, "row", [(r, r ^ 2) for r in range(4)])

    steps = jnp.array([0, 1, -1, 2] * 2, jnp.int32)
    flips = jnp.array([0] * 4 + [4] * 4, jnp.int32)
    at = jnp.concatenate([(x_hi ^ flips) + ((y + steps) & 3), tm[None], row[None]])

    def group(g):
        return lax.dynamic_slice_in_dim(right_sides, g * pair, pair, 0)

    own = jnp.concatenate([group(row ^ 3), group(row ^ 1), group(row ^ 2), group(row)], 0)
    own = own.reshape(rows, ns)
    down, up = along_y(own, 1), along_y(own, -1)
    x_own = across_x(own)
    table, total = project_first(own, at, eigen_basis)
    far = jnp.concatenate(
        [along_y(down[: rows // 2], 1), along_y(up[rows // 2 :], -1)], axis=0
    )
    x_own = after(x_own, total)
    x_down, x_up = along_y(x_own, 1), along_y(x_own, -1)
    x_far = across_x(far)
    total = project([up, down], [UP, DOWN], at, table, total)
    total = project([x_own, far], [X_OWN, FAR], at, table, total)
    total = project([x_up, x_down], [X_UP, X_DOWN], at, table, total)
    give, keep = project([x_far], [X_FAR], at, table, total, final=True)

    both = keep + other_core(give).astype(F32)
    half = pair * nt

    def part(a, k):
        return a[:, k * quarter : (k + 1) * quarter]

    to_x = both[:half].astype(BF16)
    from_x = {k: other_x(part(to_x, k)) for k in (2, 1, 3, 0)}
    times = []
    spectral = to_x
    for k in (2, 1, 3, 0):
        got = after(from_x[k], spectral)
        spectral = (part(both[half:], k) + got.astype(F32)).astype(BF16)
        spectral = spectral.reshape(pair, nt, quarter)
        times.append(along_z(spectral, k) if k else spectral)
    two, one, three, zero = times

    back = time_filter(
        [zero, one, two, three], at, noise_level, space_values, time_values, time_basis
    )
    table, loaded = load(eigen_basis, back[0])
    pieces = [back[0]] + [after(along_z(back[k], -k), loaded) for k in (1, 2, 3)]

    def assembled(parts):
        whole = jnp.zeros((pair, nt, basis), BF16)
        for k in (0, 1, 3, 2):
            whole = lax.dynamic_update_slice_in_dim(whole, parts[k], ((tm + k) & 3) * quarter, 2)
        return whole.reshape(half, basis)

    from_x = {k: other_x(pieces[k]) for k in (0, 1, 3, 2)}
    mine = assembled(pieces)
    near = jnp.concatenate([mine, other_core(mine)], 0)

    def first_step(a):
        s_up, s_down = expand([a], [X_UP, X_DOWN], at, table, ns)
        s_far = expand([a], [X_FAR], at, table, ns)
        return (along_y(s_up, 1), along_y(s_down, -1), across_x(s_far)), s_up

    steps_near, sent = first_step(near)
    from_x = assembled({k: after(a, sent) for k, a in from_x.items()})
    away = jnp.concatenate([from_x, other_core(from_x)], 0)
    steps_away, _ = first_step(away)
    fields = [after(near, *steps_near[:2]), away]
    o_up, o_down = expand(fields, [UP, DOWN], at, table, ns)
    o_up, o_down = along_y(o_up, 1), along_y(o_down, -1)
    o_x = expand(fields, [X_OWN], at, table, ns, (steps_near[:2], steps_away[:2]))
    o_x = across_x(o_x)
    o_far = expand(fields, [FAR], at, table, ns, (steps_near[2:], steps_away[2:]))
    o_far = along_y(o_far, 2)
    out = expand(fields, [OWN], at, table, ns, (), F32)
    return finish(out, at, (o_up, o_down, o_x, o_far)).reshape(rhs, nt, ns)


def solution(mesh):
    placed = (P(None, "tm", ("row", "col")), P("row", "col"), P("col"), P(), P(), P())
    return jax.shard_map(
        shards, mesh=mesh, in_specs=placed, out_specs=P(None, "tm", ("row", "col")), check_vma=False
    )
```

```python
import functools
import jax
import jax.numpy as jnp
from jax import lax
from jax.experimental import pallas as pl
from jax.experimental.pallas import tpu as pltpu
from jax.sharding import PartitionSpec as P

F32, BF16 = jnp.float32, jnp.bfloat16
COST = pl.CostEstimate(flops=1 << 10, transcendentals=0, bytes_accessed=1 << 10)
PARAMS = pltpu.CompilerParams(vmem_limit_bytes=4 << 20)
VMEM = pl.BlockSpec(memory_space=pltpu.VMEM)
SMEM = pl.BlockSpec(memory_space=pltpu.SMEM)


OWN, UP, DOWN, FAR, X_OWN, X_UP, X_DOWN, X_FAR = range(8)


def after(a, *others):
    return lax.optimization_barrier((a, *others))[0]


def rows_at(at_ref, i, ns):
    return pl.ds(pl.multiple_of(at_ref[i] * ns, ns), ns)


def project_kernel(which, final, has_total, at_ref, *refs):
    n = len(which)
    blocks, table, rest = refs[:n], refs[n], refs[n + 1 :]
    m, ns = blocks[0].shape
    width = table.shape[1]
    tile = width // 4
    for j in range(4):
        if final:
            from_lane = pl.multiple_of(((at_ref[8] + j) & 3) * tile, tile)
        else:
            from_lane = j * tile
        lanes = pl.ds(from_lane, tile)
        total = rest[0][:, lanes] if has_total else None
        for i, a in zip(which, blocks):
            term = jnp.dot(a[...], table[rows_at(at_ref, i, ns), lanes], preferred_element_type=F32)
            total = term if total is None else total + term
        to = slice(j * tile, (j + 1) * tile)
        if final:
            rest[-2][:, to] = total[: m // 2].astype(BF16)
            rest[-1][:, to] = total[m // 2 :]
        else:
            rest[-1][:, to] = total


def project(blocks, which, at, table, total=None, final=False):
    m, width = blocks[0].shape[0], table.shape[1]
    args = [at, *blocks, table] + ([] if total is None else [total])
    if final:
        out_shape = [
            jax.ShapeDtypeStruct((m // 2, width), BF16),
            jax.ShapeDtypeStruct((m // 2, width), F32),
        ]
    else:
        out_shape = jax.ShapeDtypeStruct((m, width), F32)
    return pl.pallas_call(
        functools.partial(project_kernel, which, final, total is not None),
        in_specs=[SMEM] + [VMEM] * (len(args) - 1),
        out_specs=[VMEM, VMEM] if final else VMEM,
        out_shape=out_shape,
        input_output_aliases={} if final or total is None else {len(args) - 1: 0},
        cost_estimate=COST,
        compiler_params=PARAMS,
        name="project",
    )(*args)


def first_kernel(at_ref, a_ref, basis_ref, table, total, sems):
    tile = table.shape[1] // 4
    copies = []
    for j in range(4):
        lanes = slice(j * tile, (j + 1) * tile)
        copies.append(pltpu.make_async_copy(basis_ref.at[:, lanes], table.at[:, lanes], sems.at[j]))
        copies[-1].start()
    for j in range(4):
        lanes = slice(j * tile, (j + 1) * tile)
        copies[j].wait()
        rows = rows_at(at_ref, OWN, a_ref.shape[1])
        total[:, lanes] = jnp.dot(a_ref[...], table[rows, lanes], preferred_element_type=F32)


def project_first(a, at, basis):
    return pl.pallas_call(
        first_kernel,
        in_specs=[SMEM, VMEM, pl.BlockSpec(memory_space=pl.ANY)],
        out_specs=[VMEM, VMEM],
        out_shape=[
            pltpu.VMEM(basis.shape, basis.dtype),
            jax.ShapeDtypeStruct((a.shape[0], basis.shape[1]), F32),
        ],
        scratch_shapes=[pltpu.SemaphoreType.DMA((4,))],
        cost_estimate=COST,
        compiler_params=PARAMS,
        name="project_first",
    )(at, a, basis)


def expand_kernel(which, ns, n, adds, at_ref, *refs):
    fields, table, refs = refs[:n], refs[n], refs[n + 1 :]
    m = fields[0].shape[0]
    for group, out in zip(which, refs[n * adds :]):
        row = 0
        for i in group:
            for h, a in enumerate(fields):
                value = lax.dot_general(
                    a[...],
                    table[rows_at(at_ref, i, ns), :],
                    (((1,), (1,)), ((), ())),
                    preferred_element_type=F32,
                )
                for add in refs[h * adds : (h + 1) * adds]:
                    value = value + add[:m, :].astype(F32)
                out[row : row + m, :] = value.astype(out.dtype)
                row += m


def expand(fields, which, at, table, ns, adds=(), dtype=BF16):
    rows = sum(a.shape[0] for a in fields)
    flat = [a for group in adds for a in group]
    out = pl.pallas_call(
        functools.partial(expand_kernel, which, ns, len(fields), len(flat) // len(fields)),
        in_specs=[SMEM] + [VMEM] * (len(fields) + 1 + len(flat)),
        out_specs=[VMEM] * len(which),
        out_shape=[jax.ShapeDtypeStruct((rows * len(group), ns), dtype) for group in which],
        cost_estimate=COST,
        compiler_params=PARAMS,
        name="expand",
    )(at, *fields, table, *flat)
    return out if len(which) > 1 else out[0]


def filter_kernel(nt, at_ref, noise, space, time, turn, *refs):
    ins, outs, held = refs[:4], refs[4:8], refs[8]
    rows, width = ins[0].shape
    pair = rows // nt
    z = at_ref[8]

    def times(k):
        return pl.ds(pl.multiple_of(((z - k) & 3) * nt, nt), nt)

    for k in range(4):
        for r in range(pair):
            held[times(k), r * width : (r + 1) * width] = ins[k][r * nt : (r + 1) * nt, :]
    mixed = lax.dot_general(
        turn[...], held[...], (((0,), (0,)), ((), ())), preferred_element_type=F32
    )
    space_value = space[:, pl.ds(pl.multiple_of(z * width, width), width)]
    time_value = jnp.broadcast_to(time[...], (8, time.shape[1])).T[:, :1]
    denom = space_value * time_value + noise[0]
    scaled = mixed / jnp.concatenate([denom] * pair, axis=1)
    back = jnp.dot(turn[...], scaled.astype(BF16), preferred_element_type=F32)
    held[...] = back.astype(BF16)
    for k in range(4):
        for r in range(pair):
            outs[k][r * nt : (r + 1) * nt, :] = held[times(k), r * width : (r + 1) * width]


def time_filter(parts, nt, at, noise, space, time, turn):
    rows, width = parts[0].shape
    return pl.pallas_call(
        functools.partial(filter_kernel, nt),
        in_specs=[SMEM, SMEM] + [VMEM] * 7,
        out_specs=[VMEM] * 4,
        out_shape=[jax.ShapeDtypeStruct((rows, width), BF16)] * 4,
        scratch_shapes=[pltpu.VMEM((4 * nt, rows // nt * width), BF16)],
        cost_estimate=COST,
        compiler_params=PARAMS,
        name="time_filter",
    )(at, noise, space[None, :], time[None, :], turn, *parts)


def assemble_kernel(n, at_ref, *refs):
    parts, whole, rest = refs[:n], refs[n], refs[n + 1 :]
    rows, width = parts[0].shape
    for k in range(4):
        if n == 4:
            part = parts[k][...]
            if k:
                rest[0][(k - 1) * rows : k * rows, :] = part
        else:
            part = parts[1][(k - 1) * rows : k * rows, :] if k else parts[0][...]
        whole[:, pl.ds(pl.multiple_of(((at_ref[8] + k) & 3) * width, width), width)] = part


def assemble(parts, at):
    n = len(parts)
    rows, width = parts[0].shape
    out_shape = [jax.ShapeDtypeStruct((rows, 4 * width), BF16)]
    if n == 4:
        out_shape.append(jax.ShapeDtypeStruct((3 * rows, width), BF16))
    out = pl.pallas_call(
        functools.partial(assemble_kernel, n),
        in_specs=[SMEM] + [VMEM] * n,
        out_specs=[VMEM] * len(out_shape),
        out_shape=out_shape,
        cost_estimate=COST,
        compiler_params=PARAMS,
        name="assemble",
    )(at, *parts)
    return out if n == 4 else out[0]


def finish_kernel(rows, at_ref, total, *refs):
    g, adds, out = at_ref[9], refs[:-1], refs[-1]
    n = len(adds) // 2
    for k in range(4):
        value = total[k * rows : (k + 1) * rows, :]
        for a in adds[n * (k // 2) : n * (k // 2 + 1)]:
            start = a.shape[0] - 2 * rows + (k % 2) * rows
            value = value + a[start : start + rows, :].astype(F32)
        out[pl.ds(pl.multiple_of((g ^ k) * rows, rows), rows), :] = value


def finish(total, at, adds):
    flat = [*adds[0], *adds[1]]
    return pl.pallas_call(
        functools.partial(finish_kernel, total.shape[0] // 4),
        in_specs=[SMEM] + [VMEM] * (1 + len(flat)),
        out_specs=VMEM,
        out_shape=jax.ShapeDtypeStruct(total.shape, F32),
        cost_estimate=COST,
        compiler_params=PARAMS,
        name="finish",
    )(at, total, *flat)


def shards(right_sides, eigen_basis, space_values, time_basis, time_values, noise_level):
    rhs, nt, ns = right_sides.shape
    rows = rhs * nt
    basis = space_values.shape[0]
    row, col, tm = lax.axis_index("row"), lax.axis_index("col"), lax.axis_index("tm")
    core, x_hi, y = row & 1, col & 4, col & 3
    quarter = basis // 4
    pair = rhs // 4
    eigen_basis = pltpu.with_memory_space_constraint(eigen_basis, pltpu.HBM)

    def across_x(a):
        with jax.named_scope("across_x"):
            return lax.ppermute(a, "col", [(c, c ^ 4) for c in range(8)])

    def along_y(a, k):
        with jax.named_scope("along_y%d" % (k & 3)):
            return lax.ppermute(a, "col", [(c, (c & 4) | ((c + k) & 3)) for c in range(8)])

    def along_z(a, k):
        with jax.named_scope("along_z%d" % (k & 3)):
            return lax.ppermute(a, "tm", [(z, (z + k) & 3) for z in range(4)])

    def other_core(a):
        with jax.named_scope("other_core"):
            return lax.ppermute(a, "row", [(r, r ^ 1) for r in range(4)])

    def other_x(a):
        with jax.named_scope("other_x"):
            return lax.ppermute(a, "row", [(r, r ^ 2) for r in range(4)])

    steps = jnp.array([0, 1, -1, 2] * 2, jnp.int32)
    flips = jnp.array([0] * 4 + [4] * 4, jnp.int32)
    at = jnp.concatenate([(x_hi ^ flips) + ((y + steps) & 3), tm[None], row[None]])

    def group(g):
        return lax.dynamic_slice_in_dim(right_sides, g * pair, pair, 0)

    own = jnp.concatenate([group(row ^ 3), group(row ^ 1), group(row ^ 2), group(row)], 0)
    own = own.reshape(rows, ns)
    down, up = along_y(own, 1), along_y(own, -1)
    x_own = across_x(own)
    table, total = project_first(own, at, eigen_basis)
    up, down = after(up, total), after(down, total)
    far = jnp.concatenate(
        [along_y(down[: rows // 2], 1), along_y(up[rows // 2 :], -1)], axis=0
    )
    x_own = after(x_own, total)
    x_down, x_up = along_y(x_own, 1), along_y(x_own, -1)
    x_far = across_x(far)
    total = project([up, down], [UP, DOWN], at, table, total)
    total = project([x_own, far], [X_OWN, FAR], at, table, total)
    total = project([x_up, x_down], [X_UP, X_DOWN], at, table, total)
    give, keep = project([x_far], [X_FAR], at, table, total, final=True)

    both = keep + other_core(give).astype(F32)
    half = pair * nt

    def part(a, k):
        return a[:, k * quarter : (k + 1) * quarter]

    to_x = both[:half].astype(BF16)
    from_x = {k: other_x(part(to_x, k)) for k in (2, 1, 3, 0)}
    times = []
    spectral = to_x
    for k in (2, 1, 3, 0):
        got = after(from_x[k], spectral)
        spectral = (part(both[half:], k) + got.astype(F32)).astype(BF16)
        times.append(along_z(spectral, k) if k else spectral)
    two, one, three, zero = times

    back = time_filter(
        [zero, one, two, three], nt, at, noise_level, space_values, time_values, time_basis
    )
    x_first = other_x(back[0])
    mine, rest = assemble(
        [back[0]] + [after(along_z(back[k], -k), x_first) for k in (1, 2, 3)], at
    )

    x_rest = other_x(rest)
    near = jnp.concatenate([mine, other_core(mine)], 0)

    def send(a, *which):
        return expand([a], which, at, table, ns)

    def both_ways(pair):
        return along_y(pair[0], 1), along_y(pair[1], -1)

    s_near = send(near, [X_UP], [X_DOWN])
    *o_near, f_near = send(after(near, s_near[0]), [UP], [DOWN], [X_FAR])
    sent = f_near
    s_near, o_near, f_near = both_ways(s_near), both_ways(o_near), across_x(f_near)
    from_x = assemble([x_first, after(x_rest, sent, *s_near)], at)
    away = jnp.concatenate([from_x, other_core(from_x)], 0)
    f_away = send(away, [X_FAR])
    s_away = send(after(away, f_away), [X_UP, UP], [X_DOWN, DOWN])
    sent = s_away[0]
    s_away, f_away = both_ways(s_away), across_x(f_away)

    def send_sum(a, i, adds, sent, *others):
        return expand([after(a, sent, *others)], [[i]], at, table, ns, (adds,))

    sent = f_near = send_sum(near, FAR, [f_near], sent)
    f_near = along_y(f_near, 1)
    sent = x_near = send_sum(near, X_OWN, s_near, sent, *o_near)
    x_near = across_x(x_near)
    sent = f_away = send_sum(away, FAR, [f_away], sent)
    f_away = along_y(f_away, -1)
    sent = x_away = send_sum(away, X_OWN, s_away, sent)
    x_away = across_x(x_away)
    f_near = along_y(after(f_near, sent), 1)
    f_away = along_y(after(f_away, sent), -1)
    fields = [after(near, sent, x_near), away]
    out = expand(fields, [[OWN]], at, table, ns, (), F32)
    adds = (*o_near, x_near, f_near), (*s_away, x_away, f_away)
    return finish(out, at, adds).reshape(rhs, nt, ns)


def solution(mesh):
    placed = (P(None, "tm", ("row", "col")), P("row", "col"), P("col"), P(), P(), P())
    return jax.shard_map(
        shards, mesh=mesh, in_specs=placed, out_specs=P(None, "tm", ("row", "col")), check_vma=False
    )
```

```python
import functools
import jax
import jax.numpy as jnp
from jax import lax
from jax.experimental import pallas as pl
from jax.experimental.pallas import tpu as pltpu
from jax.sharding import PartitionSpec as P

F32, BF16 = jnp.float32, jnp.bfloat16
COST = pl.CostEstimate(flops=1 << 10, transcendentals=0, bytes_accessed=1 << 10)
WORK = pl.CostEstimate(flops=1 << 30, transcendentals=0, bytes_accessed=1 << 10)
PARAMS = pltpu.CompilerParams(vmem_limit_bytes=4 << 20)
VMEM = pl.BlockSpec(memory_space=pltpu.VMEM)
SMEM = pl.BlockSpec(memory_space=pltpu.SMEM)


OWN, UP, DOWN, FAR, X_OWN, X_UP, X_DOWN, X_FAR = range(8)


def after(a, *others):
    return lax.optimization_barrier((a, *others))[0]


def rows_at(at_ref, i, ns):
    return pl.ds(pl.multiple_of(at_ref[i] * ns, ns), ns)


def project_kernel(which, at_ref, *refs):
    n = len(which)
    blocks, table, total, out = refs[:n], refs[n], refs[n + 1], refs[n + 2]
    ns = blocks[0].shape[1]
    tile = table.shape[1] // 4
    for j in range(4):
        lanes = slice(j * tile, (j + 1) * tile)
        value = total[:, lanes]
        for i, a in zip(which, blocks):
            value = value + jnp.dot(
                a[...], table[rows_at(at_ref, i, ns), lanes], preferred_element_type=F32
            )
        out[:, lanes] = value


def project(blocks, which, at, table, total):
    args = [at, *blocks, table, total]
    return pl.pallas_call(
        functools.partial(project_kernel, which),
        in_specs=[SMEM] + [VMEM] * (len(args) - 1),
        out_specs=VMEM,
        out_shape=jax.ShapeDtypeStruct(total.shape, F32),
        input_output_aliases={len(args) - 1: 0},
        cost_estimate=COST,
        compiler_params=PARAMS,
        name="project",
    )(*args)


def last_kernel(i, start, at_ref, a_ref, table, total, out):
    m, ns = out.shape[0], a_ref.shape[1]
    rows = slice(start, start + m)
    tile = table.shape[1] // 4
    for j in range(4):
        lanes = pl.ds(pl.multiple_of(((at_ref[8] + j) & 3) * tile, tile), tile)
        value = total[rows, lanes] + jnp.dot(
            a_ref[rows, :], table[rows_at(at_ref, i, ns), lanes], preferred_element_type=F32
        )
        out[:, j * tile : (j + 1) * tile] = value.astype(out.dtype)


def project_last(a, i, at, table, total, start, dtype):
    m, width = total.shape
    return pl.pallas_call(
        functools.partial(last_kernel, i, start),
        in_specs=[SMEM] + [VMEM] * 3,
        out_specs=VMEM,
        out_shape=jax.ShapeDtypeStruct((m // 2, width), dtype),
        cost_estimate=COST,
        compiler_params=PARAMS,
        name="project_last",
    )(at, a, table, total)


def first_kernel(at_ref, a_ref, basis_ref, table, total, sems):
    tile = table.shape[1] // 4
    copies = []
    for j in range(4):
        lanes = slice(j * tile, (j + 1) * tile)
        copies.append(pltpu.make_async_copy(basis_ref.at[:, lanes], table.at[:, lanes], sems.at[j]))
        copies[-1].start()
    for j in range(4):
        lanes = slice(j * tile, (j + 1) * tile)
        copies[j].wait()
        rows = rows_at(at_ref, OWN, a_ref.shape[1])
        total[:, lanes] = jnp.dot(a_ref[...], table[rows, lanes], preferred_element_type=F32)


def project_first(a, at, basis):
    return pl.pallas_call(
        first_kernel,
        in_specs=[SMEM, VMEM, pl.BlockSpec(memory_space=pl.ANY)],
        out_specs=[VMEM, VMEM],
        out_shape=[
            pltpu.VMEM(basis.shape, basis.dtype),
            jax.ShapeDtypeStruct((a.shape[0], basis.shape[1]), F32),
        ],
        scratch_shapes=[pltpu.SemaphoreType.DMA((4,))],
        cost_estimate=COST,
        compiler_params=PARAMS,
        name="project_first",
    )(at, a, basis)


def expand_kernel(which, ns, n, adds, at_ref, *refs):
    fields, table, refs = refs[:n], refs[n], refs[n + 1 :]
    m = fields[0].shape[0]
    adds = adds or (0,) * n
    lower = which == [[OWN]]
    for group, out in zip(which, refs[sum(adds) :]):
        row = 0
        for i in group:
            for h, a in enumerate(fields):
                value = lax.dot_general(
                    a[...],
                    table[rows_at(at_ref, i, ns), :],
                    (((1,), (1,)), ((), ())),
                    preferred_element_type=F32,
                )
                for add in refs[sum(adds[:h]) : sum(adds[: h + 1])]:
                    part = add[-m:, :] if lower else add[:m, :]
                    value = value + part.astype(F32)
                out[row : row + m, :] = value.astype(out.dtype)
                row += m


def expand(fields, which, at, table, ns, adds=(), dtype=BF16, cost=COST):
    rows = sum(a.shape[0] for a in fields)
    flat = [a for group in adds for a in group]
    out = pl.pallas_call(
        functools.partial(expand_kernel, which, ns, len(fields), tuple(len(group) for group in adds)),
        in_specs=[SMEM] + [VMEM] * (len(fields) + 1 + len(flat)),
        out_specs=[VMEM] * len(which),
        out_shape=[jax.ShapeDtypeStruct((rows * len(group), ns), dtype) for group in which],
        cost_estimate=cost,
        compiler_params=PARAMS,
        name="expand",
    )(at, *fields, table, *flat)
    return out if len(which) > 1 else out[0]


def filter_kernel(nt, at_ref, noise, space, time, turn, *refs):
    ins, outs, held = refs[:4], refs[4:8], refs[8]
    rows, width = ins[0].shape
    pair = rows // nt
    z = at_ref[8]

    def times(k):
        return pl.ds(pl.multiple_of(((z - k) & 3) * nt, nt), nt)

    for k in range(4):
        for r in range(pair):
            held[times(k), r * width : (r + 1) * width] = ins[k][r * nt : (r + 1) * nt, :]
    mixed = lax.dot_general(
        turn[...], held[...], (((0,), (0,)), ((), ())), preferred_element_type=F32
    )
    space_value = space[:, pl.ds(pl.multiple_of(z * width, width), width)]
    time_value = jnp.broadcast_to(time[...], (8, time.shape[1])).T[:, :1]
    denom = space_value * time_value + noise[0]
    scaled = mixed / jnp.concatenate([denom] * pair, axis=1)
    back = jnp.dot(turn[...], scaled.astype(BF16), preferred_element_type=F32)
    held[...] = back.astype(BF16)
    for k in range(4):
        for r in range(pair):
            outs[k][r * nt : (r + 1) * nt, :] = held[times(k), r * width : (r + 1) * width]


def time_filter(parts, nt, at, noise, space, time, turn):
    rows, width = parts[0].shape
    return pl.pallas_call(
        functools.partial(filter_kernel, nt),
        in_specs=[SMEM, SMEM] + [VMEM] * 7,
        out_specs=[VMEM] * 4,
        out_shape=[jax.ShapeDtypeStruct((rows, width), BF16)] * 4,
        scratch_shapes=[pltpu.VMEM((4 * nt, rows // nt * width), BF16)],
        cost_estimate=COST,
        compiler_params=PARAMS,
        name="time_filter",
    )(at, noise, space[None, :], time[None, :], turn, *parts)


def assemble_kernel(n, at_ref, *refs):
    parts, whole, rest = refs[:n], refs[n], refs[n + 1 :]
    rows, width = parts[0].shape
    for k in range(4):
        if n == 4:
            part = parts[k][...]
            if k:
                rest[0][(k - 1) * rows : k * rows, :] = part
        else:
            part = parts[1][(k - 1) * rows : k * rows, :] if k else parts[0][...]
        whole[:, pl.ds(pl.multiple_of(((at_ref[8] + k) & 3) * width, width), width)] = part


def assemble(parts, at):
    n = len(parts)
    rows, width = parts[0].shape
    out_shape = [jax.ShapeDtypeStruct((rows, 4 * width), BF16)]
    if n == 4:
        out_shape.append(jax.ShapeDtypeStruct((3 * rows, width), BF16))
    out = pl.pallas_call(
        functools.partial(assemble_kernel, n),
        in_specs=[SMEM] + [VMEM] * n,
        out_specs=[VMEM] * len(out_shape),
        out_shape=out_shape,
        cost_estimate=COST,
        compiler_params=PARAMS,
        name="assemble",
    )(at, *parts)
    return out if n == 4 else out[0]


def finish_kernel(rows, n, at_ref, total, *refs):
    g, out = at_ref[9], refs[-1]
    adds = refs[:n], refs[n:-1]
    for k in range(4):
        value = total[k * rows : (k + 1) * rows, :]
        for a in adds[k // 2]:
            value = value + a[k % 2 * rows : (k % 2 + 1) * rows, :].astype(F32)
        out[pl.ds(pl.multiple_of((g ^ k) * rows, rows), rows), :] = value


def finish(total, at, adds):
    flat = [*adds[0], *adds[1]]
    return pl.pallas_call(
        functools.partial(finish_kernel, total.shape[0] // 4, len(adds[0])),
        in_specs=[SMEM] + [VMEM] * (1 + len(flat)),
        out_specs=VMEM,
        out_shape=jax.ShapeDtypeStruct(total.shape, F32),
        cost_estimate=COST,
        compiler_params=PARAMS,
        name="finish",
    )(at, total, *flat)


def shards(right_sides, eigen_basis, space_values, time_basis, time_values, noise_level):
    rhs, nt, ns = right_sides.shape
    rows = rhs * nt
    basis = space_values.shape[0]
    row, col, tm = lax.axis_index("row"), lax.axis_index("col"), lax.axis_index("tm")
    core, x_hi, y = row & 1, col & 4, col & 3
    quarter = basis // 4
    pair = rhs // 4
    eigen_basis = pltpu.with_memory_space_constraint(eigen_basis, pltpu.HBM)

    def across_x(a):
        with jax.named_scope("across_x"):
            return lax.ppermute(a, "col", [(c, c ^ 4) for c in range(8)])

    def along_y(a, k):
        with jax.named_scope("along_y%d" % (k & 3)):
            return lax.ppermute(a, "col", [(c, (c & 4) | ((c + k) & 3)) for c in range(8)])

    def along_z(a, k):
        with jax.named_scope("along_z%d" % (k & 3)):
            return lax.ppermute(a, "tm", [(z, (z + k) & 3) for z in range(4)])

    def other_core(a):
        with jax.named_scope("other_core"):
            return lax.ppermute(a, "row", [(r, r ^ 1) for r in range(4)])

    def other_x(a):
        with jax.named_scope("other_x"):
            return lax.ppermute(a, "row", [(r, r ^ 2) for r in range(4)])

    steps = jnp.array([0, 1, -1, 2] * 2, jnp.int32)
    flips = jnp.array([0] * 4 + [4] * 4, jnp.int32)
    at = jnp.concatenate([(x_hi ^ flips) + ((y + steps) & 3), tm[None], row[None]])

    def group(g):
        return lax.dynamic_slice_in_dim(right_sides, g * pair, pair, 0)

    own = jnp.concatenate([group(row ^ 3), group(row ^ 1), group(row ^ 2), group(row)], 0)
    own = own.reshape(rows, ns)
    down, up = along_y(own, 1), along_y(own, -1)
    x_own = across_x(own)
    table, total = project_first(own, at, eigen_basis)
    up, down = after(up, total), after(down, total)
    far = jnp.concatenate(
        [along_y(down[: rows // 2], 1), along_y(up[rows // 2 :], -1)], axis=0
    )
    x_own = after(x_own, total)
    x_down, x_up = along_y(x_own, 1), along_y(x_own, -1)
    x_far = across_x(far)
    total = project([up, down], [UP, DOWN], at, table, total)
    total = project([x_own, far], [X_OWN, FAR], at, table, total)
    total = project([x_up, x_down], [X_UP, X_DOWN], at, table, total)
    give = project_last(x_far, X_FAR, at, table, total, 0, BF16)
    keep = project_last(after(x_far, give), X_FAR, at, table, total, rows // 2, F32)

    both = keep + other_core(give).astype(F32)
    half = pair * nt

    def part(a, k):
        return a[:, k * quarter : (k + 1) * quarter]

    to_x = both[:half].astype(BF16)
    from_x = {k: other_x(part(to_x, k)) for k in (2, 1, 3, 0)}
    times = []
    spectral = to_x
    for k in (2, 1, 3, 0):
        got = after(from_x[k], spectral)
        spectral = (part(both[half:], k) + got.astype(F32)).astype(BF16)
        times.append(along_z(spectral, k) if k else spectral)
    two, one, three, zero = times

    back = time_filter(
        [zero, one, two, three], nt, at, noise_level, space_values, time_values, time_basis
    )
    x_first = other_x(back[0])
    mine, rest = assemble(
        [back[0]] + [after(along_z(back[k], -k), x_first) for k in (1, 2, 3)], at
    )

    x_rest = other_x(rest)
    near = jnp.concatenate([mine, other_core(mine)], 0)

    def send(a, *which, cost=COST):
        return expand([a], which, at, table, ns, cost=cost)

    def both_ways(pair):
        return along_y(pair[0], 1), along_y(pair[1], -1)

    s_near = send(near, [X_UP], [X_DOWN], cost=WORK)
    *o_near, f_near = send(after(near, s_near[0]), [UP], [DOWN], [X_FAR], cost=WORK)
    sent = f_near
    s_near, o_near, f_near = both_ways(s_near), both_ways(o_near), across_x(f_near)
    from_x = assemble([x_first, after(x_rest, sent, *s_near)], at)
    away = jnp.concatenate([from_x, other_core(from_x)], 0)
    f_away = send(away, [X_FAR])
    s_away = send(after(away, f_away), [X_UP, UP], [X_DOWN, DOWN])
    sent = s_away[0]
    s_away, f_away = both_ways(s_away), across_x(f_away)

    def send_sum(a, i, adds, sent, *others):
        return expand([after(a, sent, *others)], [[i]], at, table, ns, (adds,))

    sent = f_near = send_sum(near, FAR, [f_near], sent)
    f_near = along_y(f_near, 1)
    sent = x_near = send_sum(near, X_OWN, s_near, sent, *o_near)
    x_near = across_x(x_near)
    sent = f_away = send_sum(away, FAR, [f_away], sent)
    f_away = along_y(f_away, -1)
    sent = x_away = send_sum(away, X_OWN, s_away, sent)
    x_away = across_x(x_away)
    f_near = along_y(after(f_near, sent), 1)
    f_away = along_y(after(f_away, sent), -1)
    fields = [after(near, sent), away]
    early = (*o_near, x_near), s_away
    out = expand(fields, [[OWN]], at, table, ns, early, F32)
    adds = (f_near,), (x_away, f_away)
    return finish(out, at, adds).reshape(rhs, nt, ns)


def solution(mesh):
    placed = (P(None, "tm", ("row", "col")), P("row", "col"), P("col"), P(), P(), P())
    return jax.shard_map(
        shards, mesh=mesh, in_specs=placed, out_specs=P(None, "tm", ("row", "col")), check_vma=False
    )
```

```python
import functools
import jax
import jax.numpy as jnp
from jax import lax
from jax.experimental import pallas as pl
from jax.experimental.pallas import tpu as pltpu
from jax.sharding import PartitionSpec as P

F32, BF16 = jnp.float32, jnp.bfloat16
COST = pl.CostEstimate(flops=1 << 10, transcendentals=0, bytes_accessed=1 << 10)
WORK = pl.CostEstimate(flops=1 << 30, transcendentals=0, bytes_accessed=1 << 10)
PARAMS = pltpu.CompilerParams(vmem_limit_bytes=4 << 20)
VMEM = pl.BlockSpec(memory_space=pltpu.VMEM)
SMEM = pl.BlockSpec(memory_space=pltpu.SMEM)


OWN, UP, DOWN, FAR, X_OWN, X_UP, X_DOWN, X_FAR = range(8)


def after(a, *others):
    return lax.optimization_barrier((a, *others))[0]


def rows_at(at_ref, i, ns):
    return pl.ds(pl.multiple_of(at_ref[i] * ns, ns), ns)


def project_kernel(which, at_ref, *refs):
    n = len(which)
    blocks, table, total, out = refs[:n], refs[n], refs[n + 1], refs[n + 2]
    ns = blocks[0].shape[1]
    tile = table.shape[1] // 4
    for j in range(4):
        lanes = slice(j * tile, (j + 1) * tile)
        value = total[:, lanes]
        for i, a in zip(which, blocks):
            value = value + jnp.dot(
                a[...], table[rows_at(at_ref, i, ns), lanes], preferred_element_type=F32
            )
        out[:, lanes] = value


def project(blocks, which, at, table, total):
    args = [at, *blocks, table, total]
    return pl.pallas_call(
        functools.partial(project_kernel, which),
        in_specs=[SMEM] + [VMEM] * (len(args) - 1),
        out_specs=VMEM,
        out_shape=jax.ShapeDtypeStruct(total.shape, F32),
        input_output_aliases={len(args) - 1: 0},
        cost_estimate=COST,
        compiler_params=PARAMS,
        name="project",
    )(*args)


def last_kernel(i, places, at_ref, a_ref, table, total, out):
    m, ns = out.shape[0] // len(places), a_ref.shape[1]
    tile = table.shape[1] // 4
    groups = [pl.ds(pl.multiple_of((at_ref[9] ^ p) * m, m), m) for p in places]
    a = jnp.concatenate([a_ref[rows, :] for rows in groups], axis=0)
    for j in range(4):
        lanes = pl.ds(pl.multiple_of(((at_ref[8] + j) & 3) * tile, tile), tile)
        value = jnp.dot(a, table[rows_at(at_ref, i, ns), lanes], preferred_element_type=F32)
        value = value + jnp.concatenate([total[rows, lanes] for rows in groups], axis=0)
        out[:, j * tile : (j + 1) * tile] = value.astype(out.dtype)


def project_last(a, i, at, table, total, places, dtype):
    m, width = total.shape
    return pl.pallas_call(
        functools.partial(last_kernel, i, places),
        in_specs=[SMEM] + [VMEM] * 3,
        out_specs=VMEM,
        out_shape=jax.ShapeDtypeStruct((m // 4 * len(places), width), dtype),
        cost_estimate=COST,
        compiler_params=PARAMS,
        name="project_last",
    )(at, a, table, total)


def first_kernel(at_ref, a_ref, basis_ref, table, total, sems):
    tile = table.shape[1] // 4
    copies = []
    for j in range(4):
        lanes = slice(j * tile, (j + 1) * tile)
        copies.append(pltpu.make_async_copy(basis_ref.at[:, lanes], table.at[:, lanes], sems.at[j]))
        copies[-1].start()
    for j in range(4):
        lanes = slice(j * tile, (j + 1) * tile)
        copies[j].wait()
        rows = rows_at(at_ref, OWN, a_ref.shape[1])
        total[:, lanes] = jnp.dot(a_ref[...], table[rows, lanes], preferred_element_type=F32)


def project_first(a, at, basis):
    return pl.pallas_call(
        first_kernel,
        in_specs=[SMEM, VMEM, pl.BlockSpec(memory_space=pl.ANY)],
        out_specs=[VMEM, VMEM],
        out_shape=[
            pltpu.VMEM(basis.shape, basis.dtype),
            jax.ShapeDtypeStruct((a.shape[0], basis.shape[1]), F32),
        ],
        scratch_shapes=[pltpu.SemaphoreType.DMA((4,))],
        cost_estimate=COST,
        compiler_params=PARAMS,
        name="project_first",
    )(at, a, basis)


def expand_kernel(which, ns, n, adds, at_ref, *refs):
    fields, table, refs = refs[:n], refs[n], refs[n + 1 :]
    m = fields[0].shape[0]
    adds = adds or (0,) * n
    lower = which == [[OWN]]
    for group, out in zip(which, refs[sum(adds) :]):
        row = 0
        for i in group:
            for h, a in enumerate(fields):
                value = lax.dot_general(
                    a[...],
                    table[rows_at(at_ref, i, ns), :],
                    (((1,), (1,)), ((), ())),
                    preferred_element_type=F32,
                )
                for add in refs[sum(adds[:h]) : sum(adds[: h + 1])]:
                    part = add[-m:, :] if lower else add[:m, :]
                    value = value + part.astype(F32)
                out[row : row + m, :] = value.astype(out.dtype)
                row += m


def expand(fields, which, at, table, ns, adds=(), dtype=BF16, cost=COST):
    rows = sum(a.shape[0] for a in fields)
    flat = [a for group in adds for a in group]
    out = pl.pallas_call(
        functools.partial(expand_kernel, which, ns, len(fields), tuple(len(group) for group in adds)),
        in_specs=[SMEM] + [VMEM] * (len(fields) + 1 + len(flat)),
        out_specs=[VMEM] * len(which),
        out_shape=[jax.ShapeDtypeStruct((rows * len(group), ns), dtype) for group in which],
        cost_estimate=cost,
        compiler_params=PARAMS,
        name="expand",
    )(at, *fields, table, *flat)
    return out if len(which) > 1 else out[0]


def filter_kernel(nt, at_ref, noise, space, time, turn, *refs):
    ins, outs, held = refs[:4], refs[4:8], refs[8]
    rows, width = ins[0].shape
    pair = rows // nt
    z = at_ref[8]

    def times(k):
        return pl.ds(pl.multiple_of(((z - k) & 3) * nt, nt), nt)

    for k in range(4):
        for r in range(pair):
            held[times(k), r * width : (r + 1) * width] = ins[k][r * nt : (r + 1) * nt, :]
    mixed = lax.dot_general(
        turn[...], held[...], (((0,), (0,)), ((), ())), preferred_element_type=F32
    )
    space_value = space[:, pl.ds(pl.multiple_of(z * width, width), width)]
    time_value = jnp.broadcast_to(time[...], (8, time.shape[1])).T[:, :1]
    denom = space_value * time_value + noise[0]
    scaled = mixed / jnp.concatenate([denom] * pair, axis=1)
    back = jnp.dot(turn[...], scaled.astype(BF16), preferred_element_type=F32)
    held[...] = back.astype(BF16)
    for k in range(4):
        for r in range(pair):
            outs[k][r * nt : (r + 1) * nt, :] = held[times(k), r * width : (r + 1) * width]


def time_filter(parts, nt, at, noise, space, time, turn):
    rows, width = parts[0].shape
    return pl.pallas_call(
        functools.partial(filter_kernel, nt),
        in_specs=[SMEM, SMEM] + [VMEM] * 7,
        out_specs=[VMEM] * 4,
        out_shape=[jax.ShapeDtypeStruct((rows, width), BF16)] * 4,
        scratch_shapes=[pltpu.VMEM((4 * nt, rows // nt * width), BF16)],
        cost_estimate=COST,
        compiler_params=PARAMS,
        name="time_filter",
    )(at, noise, space[None, :], time[None, :], turn, *parts)


def assemble_kernel(n, at_ref, *refs):
    parts, whole, rest = refs[:n], refs[n], refs[n + 1 :]
    rows, width = parts[0].shape
    for k in range(4):
        if n == 4:
            part = parts[k][...]
            if k:
                rest[0][(k - 1) * rows : k * rows, :] = part
        else:
            part = parts[1][(k - 1) * rows : k * rows, :] if k else parts[0][...]
        whole[:, pl.ds(pl.multiple_of(((at_ref[8] + k) & 3) * width, width), width)] = part


def assemble(parts, at):
    n = len(parts)
    rows, width = parts[0].shape
    out_shape = [jax.ShapeDtypeStruct((rows, 4 * width), BF16)]
    if n == 4:
        out_shape.append(jax.ShapeDtypeStruct((3 * rows, width), BF16))
    out = pl.pallas_call(
        functools.partial(assemble_kernel, n),
        in_specs=[SMEM] + [VMEM] * n,
        out_specs=[VMEM] * len(out_shape),
        out_shape=out_shape,
        cost_estimate=COST,
        compiler_params=PARAMS,
        name="assemble",
    )(at, *parts)
    return out if n == 4 else out[0]


def finish_kernel(rows, n, at_ref, total, *refs):
    g, out = at_ref[9], refs[-1]
    adds = refs[:n], refs[n:-1]
    for k in range(4):
        value = total[k * rows : (k + 1) * rows, :]
        for a in adds[k // 2]:
            value = value + a[k % 2 * rows : (k % 2 + 1) * rows, :].astype(F32)
        out[pl.ds(pl.multiple_of((g ^ k) * rows, rows), rows), :] = value


def finish(total, at, adds):
    flat = [*adds[0], *adds[1]]
    return pl.pallas_call(
        functools.partial(finish_kernel, total.shape[0] // 4, len(adds[0])),
        in_specs=[SMEM] + [VMEM] * (1 + len(flat)),
        out_specs=VMEM,
        out_shape=jax.ShapeDtypeStruct(total.shape, F32),
        cost_estimate=COST,
        compiler_params=PARAMS,
        name="finish",
    )(at, total, *flat)


def shards(right_sides, eigen_basis, space_values, time_basis, time_values, noise_level):
    rhs, nt, ns = right_sides.shape
    rows = rhs * nt
    basis = space_values.shape[0]
    row, col, tm = lax.axis_index("row"), lax.axis_index("col"), lax.axis_index("tm")
    core, x_hi, y = row & 1, col & 4, col & 3
    quarter = basis // 4
    pair = rhs // 4
    eigen_basis = pltpu.with_memory_space_constraint(eigen_basis, pltpu.HBM)

    def across_x(a):
        with jax.named_scope("across_x"):
            return lax.ppermute(a, "col", [(c, c ^ 4) for c in range(8)])

    def along_y(a, k):
        with jax.named_scope("along_y%d" % (k & 3)):
            return lax.ppermute(a, "col", [(c, (c & 4) | ((c + k) & 3)) for c in range(8)])

    def along_z(a, k):
        with jax.named_scope("along_z%d" % (k & 3)):
            return lax.ppermute(a, "tm", [(z, (z + k) & 3) for z in range(4)])

    def other_core(a):
        with jax.named_scope("other_core"):
            return lax.ppermute(a, "row", [(r, r ^ 1) for r in range(4)])

    def other_x(a):
        with jax.named_scope("other_x"):
            return lax.ppermute(a, "row", [(r, r ^ 2) for r in range(4)])

    steps = jnp.array([0, 1, -1, 2] * 2, jnp.int32)
    flips = jnp.array([0] * 4 + [4] * 4, jnp.int32)
    at = jnp.concatenate([(x_hi ^ flips) + ((y + steps) & 3), tm[None], row[None]])

    own = right_sides.reshape(rows, ns)
    down, up = along_y(own, 1), along_y(own, -1)
    x_own = across_x(own)
    table, total = project_first(own, at, eigen_basis)
    up, down = after(up, total), after(down, total)
    far = jnp.concatenate(
        [along_y(down[: rows // 2], 1), along_y(up[rows // 2 :], -1)], axis=0
    )
    x_own = after(x_own, total)
    x_down, x_up = along_y(x_own, 1), along_y(x_own, -1)
    x_far = across_x(far)
    total = project([up, down], [UP, DOWN], at, table, total)
    total = project([x_own, far], [X_OWN, FAR], at, table, total)
    total = project([x_up, x_down], [X_UP, X_DOWN], at, table, total)
    give = project_last(x_far, X_FAR, at, table, total, (3, 1), BF16)
    keep = project_last(after(x_far, give), X_FAR, at, table, total, (2, 0), F32)

    both = keep + other_core(give).astype(F32)
    half = pair * nt

    def part(a, k):
        return a[:, k * quarter : (k + 1) * quarter]

    to_x = both[:half].astype(BF16)
    from_x = {k: other_x(part(to_x, k)) for k in (2, 1, 3, 0)}
    times = []
    spectral = to_x
    for k in (2, 1, 3, 0):
        got = after(from_x[k], spectral)
        spectral = (part(both[half:], k) + got.astype(F32)).astype(BF16)
        times.append(along_z(spectral, k) if k else spectral)
    two, one, three, zero = times

    back = time_filter(
        [zero, one, two, three], nt, at, noise_level, space_values, time_values, time_basis
    )
    x_first = other_x(back[0])
    mine, rest = assemble(
        [back[0]] + [after(along_z(back[k], -k), x_first) for k in (1, 2, 3)], at
    )

    x_rest = other_x(rest)
    near = jnp.concatenate([mine, other_core(mine)], 0)

    def send(a, *which, cost=COST):
        return expand([a], which, at, table, ns, cost=cost)

    def both_ways(pair):
        return along_y(pair[0], 1), along_y(pair[1], -1)

    s_near = send(near, [X_UP], [X_DOWN], cost=WORK)
    *o_near, f_near = send(after(near, s_near[0]), [UP], [DOWN], [X_FAR], cost=WORK)
    sent = f_near
    s_near, o_near, f_near = both_ways(s_near), both_ways(o_near), across_x(f_near)
    from_x = assemble([x_first, after(x_rest, sent, *s_near)], at)
    away = jnp.concatenate([from_x, other_core(from_x)], 0)
    f_away = send(away, [X_FAR])
    s_away = send(after(away, f_away), [X_UP, UP], [X_DOWN, DOWN])
    sent = s_away[0]
    s_away, f_away = both_ways(s_away), across_x(f_away)

    def send_sum(a, i, adds, sent, *others):
        return expand([after(a, sent, *others)], [[i]], at, table, ns, (adds,))

    sent = f_near = send_sum(near, FAR, [f_near], sent)
    f_near = along_y(f_near, 1)
    sent = x_near = send_sum(near, X_OWN, s_near, sent, *o_near)
    x_near = across_x(x_near)
    sent = f_away = send_sum(away, FAR, [f_away], sent)
    f_away = along_y(f_away, -1)
    sent = x_away = send_sum(away, X_OWN, s_away, sent)
    x_away = across_x(x_away)
    f_near = along_y(after(f_near, sent), 1)
    f_away = along_y(after(f_away, sent), -1)
    fields = [after(near, sent), away]
    early = (*o_near, x_near), s_away
    out = expand(fields, [[OWN]], at, table, ns, early, F32)
    adds = (f_near,), (x_away, f_away)
    return finish(out, at, adds).reshape(rhs, nt, ns)


def solution(mesh):
    placed = (P(None, "tm", ("row", "col")), P("row", "col"), P("col"), P(), P(), P())
    return jax.shard_map(
        shards, mesh=mesh, in_specs=placed, out_specs=P(None, "tm", ("row", "col")), check_vma=False
    )
```
